32 devices in a mesh: frames: 2 (over core), heads: 4 (over y, x), dp: 4 (over z).
Axes of the slice: x: 2, y: 2, z: 4, core: 2. Of those that a mesh axis runs over, the one named last changes fastest.
Arguments:
- queries: bfloat16 [1280, 4096], P(('dp', 'frames'), 'heads'), parts along dimension 0, may hold values from -10 to 10
- key_vectors: bfloat16 [1280, 4096], P(('dp', 'frames'), 'heads'), parts along dimension 0, may hold values from -4 to 4
- values: bfloat16 [1280, 4096], P(('dp', 'frames'), 'heads'), parts along dimension 0, may hold values from -5 to 5
- grad_output: bfloat16 [1280, 4096], P(('dp', 'frames'), 'heads'), parts along dimension 0, may hold values from -5 to 5
- segment_index: int32 [1280], P(('dp', 'frames')), parts along dimension 0, may hold values from 0 to 7, as said below
Outputs:
- attended: bfloat16 [1280, 4096], P(('dp', 'frames'), 'heads'), parts along dimension 0
- grad_queries: bfloat16 [1280, 4096], P(('dp', 'frames'), 'heads'), parts along dimension 0
- grad_keys: bfloat16 [1280, 4096], P(('dp', 'frames'), 'heads'), parts along dimension 0
- grad_values: bfloat16 [1280, 4096], P(('dp', 'frames'), 'heads'), parts along dimension 0
The draws below stay inside these ranges and needn't reach their ends.
There are 4 independent parts, one for each index of `dp`. The reference program is written for one: setup_inputs(seed, part) draws one part's arguments, and reference() takes and returns one part's arrays. A program takes and returns all parts, laid end to end along the dimension named above; each array names one. Nothing has to cross between parts.
Inputs may be any that keep to these rules, and one draw needn't show every extreme that they name: `segment_index`: rows are stored in paired order: the first 80 rows of frames index g are the natural positions g * 80 onward, its last 80 rows the positions (3 - g) * 80 onward. Along natural positions the segment never falls, starts at 0 (the reference-image prefix), and each of the 8 segments holds at least one position.
All inputs are finite; a program needn't handle non-finite values.
Results may differ from the reference program's by a relative error of at most 0.014.
Values may be sent and summed in bfloat16 or wider, within the bound.
No kernel may reach another device: no remote copies, remote signals or barrier semaphores. Data moves between devices by JAX's collectives and lax.ppermute only.
A program may use at most 128 MiB of HBM per device.

```python
import math
import jax
import jax.numpy as jnp
from jax import lax

HEADS = 32
HEAD_DIM = 128
TOK_DEV = 160
TOKENS = 320
GROUPS = 8
BLOCKS = 4
HALF = 80


def drawn_pair(key):
    shape = (TOKENS, HEADS * HEAD_DIM)
    query_rows = jax.random.truncated_normal(jax.random.fold_in(key, 36), -4.0, 4.0, shape)
    key_rows = jax.random.truncated_normal(jax.random.fold_in(key, 37), -4.0, 4.0, shape)
    return (query_rows.astype(jnp.float32), key_rows.astype(jnp.float32))


def draw_queries(key, part):
    return drawn_pair(key)[0].astype(jnp.bfloat16)


def draw_key_vectors(key, part):
    return drawn_pair(key)[1].astype(jnp.bfloat16)


def draw_segment_index(key, part):
    cuts = jax.random.permutation(jax.random.fold_in(key, 21), TOKENS - 1)[:GROUPS - 1] + 1
    positions = jnp.arange(TOKENS)
    natural = jnp.sum((cuts[None, :] <= positions[:, None]).astype(jnp.int32), axis=1).astype(jnp.int32)
    owner = positions // TOK_DEV
    inside = positions % TOK_DEV
    half_block = jnp.where(inside // HALF == 0, owner, BLOCKS - 1 - owner)
    natural_pos = (half_block * HALF + inside % HALF).astype(jnp.int32)
    return natural[natural_pos].astype(jnp.int32)


def steps_of(key, dims, split, low, top_value):
    def one(axis_at, parts):
        draws = jax.random.uniform(jax.random.fold_in(jax.random.fold_in(key, 6), axis_at), (parts,), jnp.float32, low / len(split), top_value / len(split))
        return jnp.repeat(jnp.exp(draws), dims[axis_at] // parts).reshape((-1,) + (1,) * (len(dims) - axis_at - 1))

    factor_of = one(*split[0])
    for cut in split[1:]:
        factor_of = factor_of * one(*cut)
    return factor_of


def scatter_about(own_key, extent, width, most, pieces=(), held_as=jnp.bfloat16):
    values = width * jax.random.normal(own_key, extent, jnp.float32)
    if pieces:
        values = values * steps_of(own_key, extent, pieces, -0.22, 0.18)
    return jnp.clip(values, -most, most).astype(held_as)


def setup_inputs(seed: int = 0, part: int = 0) -> dict:
    streams_of = jax.random.split(jax.random.key(seed), 6)
    own_keys = jax.random.split(jax.random.fold_in(streams_of[5], part), 6)
    queries = draw_queries(jax.random.fold_in(jax.random.fold_in(streams_of[5], part), 71), part)
    key_vectors = draw_key_vectors(jax.random.fold_in(jax.random.fold_in(streams_of[5], part), 71), part)
    values = scatter_about(own_keys[2], (TOKENS, HEADS * HEAD_DIM), 1.0, 5.0, ((0, 2), (1, 4)))
    grad_output = scatter_about(own_keys[3], (TOKENS, HEADS * HEAD_DIM), 1.0, 5.0, ((0, 2), (1, 4)))
    segment_index = draw_segment_index(jax.random.fold_in(jax.random.fold_in(streams_of[5], part), 71), part)
    return dict(queries=queries, key_vectors=key_vectors, values=values, grad_output=grad_output, segment_index=segment_index)


def reference(queries, key_vectors, values, grad_output, segment_index):
    scale_factor = 1.0 / math.sqrt(HEAD_DIM)
    seen_mask = segment_index[None, :] <= segment_index[:, None]

    def split_heads(array):
        return array.reshape(TOKENS, HEADS, HEAD_DIM).transpose(1, 0, 2)

    def merge_heads(array):
        return array.transpose(1, 0, 2).reshape(TOKENS, HEADS * HEAD_DIM)

    def one_head(items):
        query_head, key_head, value_head, grad_head = items
        scores = jnp.dot(query_head, key_head.T, preferred_element_type=jnp.float32) * scale_factor
        row_max = lax.optimization_barrier(jnp.max(jnp.where(seen_mask, scores, -jnp.inf), axis=1, keepdims=True))
        exp_sum = lax.optimization_barrier(jnp.sum(jnp.where(seen_mask, jnp.exp(scores - row_max), 0.0), axis=1, keepdims=True))
        log_total = row_max + jnp.log(exp_sum)
        soft_weights = jnp.where(seen_mask, jnp.exp(scores - log_total), 0.0)
        weights_low = soft_weights.astype(jnp.bfloat16)
        attended = jnp.dot(weights_low, value_head, preferred_element_type=jnp.float32).astype(jnp.bfloat16)
        row_delta = lax.optimization_barrier(jnp.sum(grad_head.astype(jnp.float32) * attended.astype(jnp.float32), axis=1, keepdims=True))
        grad_weights = jnp.dot(grad_head, value_head.T, preferred_element_type=jnp.float32)
        grad_scores = (soft_weights * (grad_weights - row_delta)).astype(jnp.bfloat16)
        grad_query = (jnp.dot(grad_scores, key_head, preferred_element_type=jnp.float32) * scale_factor).astype(jnp.bfloat16)
        grad_key = (jnp.dot(grad_scores.T, query_head, preferred_element_type=jnp.float32) * scale_factor).astype(jnp.bfloat16)
        grad_value = jnp.dot(weights_low.T, grad_head, preferred_element_type=jnp.float32).astype(jnp.bfloat16)
        return (attended, grad_query, grad_key, grad_value)
    results = lax.map(one_head, (split_heads(queries), split_heads(key_vectors), split_heads(values), split_heads(grad_output)))
    return (merge_heads(results[0]), merge_heads(results[1]), merge_heads(results[2]), merge_heads(results[3]))
```

```python
import functools
import math

import jax
import jax.numpy as jnp
from jax import lax
from jax.experimental import pallas as pl
from jax.experimental.pallas import tpu as pltpu
from jax.sharding import PartitionSpec as P

HEAD_DIM = 128


def head_split(array):
    return array.reshape(array.shape[0], array.shape[1] // HEAD_DIM, HEAD_DIM)


def natural_order(array, shard_count, row_count):
    half_rows = row_count // 2
    parts = array.reshape((shard_count, 2, half_rows) + array.shape[1:])
    joined = jnp.concatenate([parts[:, 0], jnp.flip(parts[:, 1], axis=0)], axis=0)
    return joined.reshape((shard_count * row_count,) + array.shape[1:])


def score_block(query_heads, key_heads):
    product = jnp.einsum("qhd,khd->qhk", query_heads, key_heads, preferred_element_type=jnp.float32)
    return product * (1.0 / math.sqrt(HEAD_DIM))


def visible(query_segment, key_segment):
    return key_segment[None, None, :] <= query_segment[:, None, None]


def weights_of(query_heads, query_segment, log_total, key_heads, key_segment):
    scores = score_block(query_heads, key_heads)
    return jnp.where(
        visible(query_segment, key_segment), jnp.exp(scores - log_total[:, :, None]), 0.0
    )


def grad_parts(
    query_heads,
    grad_heads,
    query_segment,
    log_total,
    row_delta,
    key_heads,
    value_heads,
    key_segment,
):
    soft_weights = weights_of(query_heads, query_segment, log_total, key_heads, key_segment)
    grad_weights = jnp.einsum(
        "qhd,khd->qhk", grad_heads, value_heads, preferred_element_type=jnp.float32
    )
    grad_scores = (soft_weights * (grad_weights - row_delta[:, :, None])).astype(jnp.bfloat16)
    return (soft_weights.astype(jnp.bfloat16), grad_scores)


def shards(queries, key_vectors, values, grad_output, segment_index):
    row_count, full_width = queries.shape
    head_count = full_width // HEAD_DIM
    shard_count = lax.axis_size("frames")
    scale_factor = 1.0 / math.sqrt(HEAD_DIM)
    query_heads = head_split(queries)
    grad_heads = head_split(grad_output)
    own_segment = segment_index.astype(jnp.float32)
    own_top = jnp.max(own_segment)
    own_bottom = jnp.min(own_segment)
    segment_tags = segment_index.astype(jnp.bfloat16)
    key_whole, value_whole, key_tags = (
        lax.all_gather(key_vectors, "frames", axis=0, tiled=True),
        lax.all_gather(values, "frames", axis=0, tiled=True),
        lax.all_gather(segment_tags, "frames", axis=0, tiled=True),
    )
    key_total = key_whole.shape[0]
    key_span = min(key_total, 4 * row_count)
    span_count = key_total // key_span
    key_heads_all = head_split(natural_order(key_whole, shard_count, row_count))
    value_heads_all = head_split(natural_order(value_whole, shard_count, row_count))
    key_segment_all = natural_order(key_tags, shard_count, row_count).astype(jnp.float32)

    def key_slice(block_index):
        first_row = block_index * key_span
        return (
            lax.dynamic_slice_in_dim(key_heads_all, first_row, key_span, 0),
            lax.dynamic_slice_in_dim(value_heads_all, first_row, key_span, 0),
            lax.dynamic_slice_in_dim(key_segment_all, first_row, key_span, 0),
        )

    def span_seen(key_segment):
        return jnp.min(key_segment) <= own_top

    def stats_step(block_index, loop_state):
        key_heads, value_heads, key_segment = key_slice(block_index)

        def stats_work(state):
            running_max, running_sum = state
            seen_mask = visible(own_segment, key_segment)
            scores = jnp.where(seen_mask, score_block(query_heads, key_heads), -1e30)
            new_max = jnp.maximum(running_max, jnp.max(scores, axis=2))
            added = jnp.sum(
                jnp.where(seen_mask, jnp.exp(scores - new_max[:, :, None]), 0.0), axis=2
            )
            return (new_max, running_sum * jnp.exp(running_max - new_max) + added)

        return lax.cond(span_seen(key_segment), stats_work, lambda state: state, loop_state)

    start_max = jnp.full((row_count, head_count), -1e30, jnp.float32)
    start_sum = jnp.zeros((row_count, head_count), jnp.float32)
    running_max, running_sum = lax.fori_loop(0, span_count, stats_step, (start_max, start_sum))
    log_total = running_max + jnp.log(running_sum)

    def output_step(block_index, total_acc):
        key_heads, value_heads, key_segment = key_slice(block_index)

        def output_work(acc):
            weights_low = weights_of(
                query_heads, own_segment, log_total, key_heads, key_segment
            ).astype(jnp.bfloat16)
            return acc + jnp.einsum(
                "qhk,khd->qhd", weights_low, value_heads, preferred_element_type=jnp.float32
            )

        return lax.cond(span_seen(key_segment), output_work, lambda acc: acc, total_acc)

    zero_rows = jnp.zeros((row_count, head_count, HEAD_DIM), jnp.float32)
    attended = (
        lax.fori_loop(0, span_count, output_step, zero_rows)
        .reshape(row_count, full_width)
        .astype(jnp.bfloat16)
    )
    row_delta = jnp.sum(
        grad_heads.astype(jnp.float32) * head_split(attended).astype(jnp.float32), axis=2
    )

    def query_grad_step(block_index, total_acc):
        key_heads, value_heads, key_segment = key_slice(block_index)

        def query_work(acc):
            weights_low, grad_scores = grad_parts(
                query_heads,
                grad_heads,
                own_segment,
                log_total,
                row_delta,
                key_heads,
                value_heads,
                key_segment,
            )
            return acc + jnp.einsum(
                "qhk,khd->qhd", grad_scores, key_heads, preferred_element_type=jnp.float32
            )

        return lax.cond(span_seen(key_segment), query_work, lambda acc: acc, total_acc)

    query_acc = lax.fori_loop(0, span_count, query_grad_step, zero_rows)
    grad_queries = (query_acc * scale_factor).reshape(row_count, full_width).astype(jnp.bfloat16)
    query_whole, grad_whole, query_tags = (
        lax.all_gather(queries, "frames", axis=0, tiled=True),
        lax.all_gather(grad_output, "frames", axis=0, tiled=True),
        lax.all_gather(segment_tags, "frames", axis=0, tiled=True),
    )
    total_whole, delta_whole = (
        lax.all_gather(log_total, "frames", axis=0, tiled=True),
        lax.all_gather(row_delta, "frames", axis=0, tiled=True),
    )
    query_heads_all = head_split(natural_order(query_whole, shard_count, row_count))
    grad_heads_all = head_split(natural_order(grad_whole, shard_count, row_count))
    query_segment_all = natural_order(query_tags, shard_count, row_count).astype(jnp.float32)
    total_all = natural_order(total_whole, shard_count, row_count)
    delta_all = natural_order(delta_whole, shard_count, row_count)
    own_keys = head_split(key_vectors)
    own_values = head_split(values)

    def key_grad_step(block_index, loop_state):
        first_row = block_index * key_span
        block_queries = lax.dynamic_slice_in_dim(query_heads_all, first_row, key_span, 0)
        block_grads = lax.dynamic_slice_in_dim(grad_heads_all, first_row, key_span, 0)
        block_segment = lax.dynamic_slice_in_dim(query_segment_all, first_row, key_span, 0)
        block_total = lax.dynamic_slice_in_dim(total_all, first_row, key_span, 0)
        block_delta = lax.dynamic_slice_in_dim(delta_all, first_row, key_span, 0)

        def key_work(state):
            key_acc, value_acc = state
            weights_low, grad_scores = grad_parts(
                block_queries,
                block_grads,
                block_segment,
                block_total,
                block_delta,
                own_keys,
                own_values,
                own_segment,
            )
            key_acc = key_acc + jnp.einsum(
                "qhk,qhd->khd", grad_scores, block_queries, preferred_element_type=jnp.float32
            )
            value_acc = value_acc + jnp.einsum(
                "qhk,qhd->khd", weights_low, block_grads, preferred_element_type=jnp.float32
            )
            return (key_acc, value_acc)

        return lax.cond(
            jnp.max(block_segment) >= own_bottom, key_work, lambda state: state, loop_state
        )

    key_acc, value_acc = lax.fori_loop(0, span_count, key_grad_step, (zero_rows, zero_rows))
    grad_keys = (key_acc * scale_factor).reshape(row_count, full_width).astype(jnp.bfloat16)
    grad_values = value_acc.reshape(row_count, full_width).astype(jnp.bfloat16)
    return (attended, grad_queries, grad_keys, grad_values)


HIDDEN = -1e30
NT = (((1,), (1,)), ((), ()))
TN = (((0,), (0,)), ((), ()))
NN = (((1,), (0,)), ((), ()))


def dot(left, right, dims):
    return lax.dot_general(left, right, dims, preferred_element_type=jnp.float32)


def pair_kernel(
    head_count, row_count, bias_ref, q0, k0, v0, g0, q1, k1, v1, g1, o_ref, dq_ref, dk_ref, dv_ref
):
    scale = 1.0 / math.sqrt(HEAD_DIM)
    for head in range(head_count):
        cols = slice(head * HEAD_DIM, (head + 1) * HEAD_DIM)
        q = jnp.concatenate([q0[:, cols], q1[:, cols]], axis=0)
        k = jnp.concatenate([k0[:, cols], k1[:, cols]], axis=0)
        v = jnp.concatenate([v0[:, cols], v1[:, cols]], axis=0)
        g = jnp.concatenate([g0[:, cols], g1[:, cols]], axis=0)
        scores = dot(k, q, NT) + bias_ref[...]
        top = jnp.max(scores, axis=0, keepdims=True)
        raw = jnp.exp((scores - top) * scale)
        soft = raw * (1.0 / jnp.sum(raw, axis=0, keepdims=True))
        low = soft.astype(jnp.bfloat16)
        grad_weights = dot(v, g, NT)
        product = soft * grad_weights
        delta = jnp.sum(product, axis=0, keepdims=True)
        grad_scores = (product - soft * delta).astype(jnp.bfloat16)
        o_ref[:, cols] = dot(low[:, :row_count], v, TN).astype(jnp.bfloat16)
        dq_ref[:, cols] = (dot(grad_scores[:, :row_count], k, TN) * scale).astype(jnp.bfloat16)
        dk_ref[:, cols] = (dot(grad_scores[:row_count], q, NN) * scale).astype(jnp.bfloat16)
        dv_ref[:, cols] = dot(low[:row_count], g, NN).astype(jnp.bfloat16)


def pair_body(queries, key_vectors, values, grad_output, segment_index):
    row_count, width = queries.shape

    def swap(array):
        return lax.ppermute(array, "frames", [(0, 1), (1, 0)])

    other_segment = swap(segment_index)
    other_queries, other_keys = swap(queries), swap(key_vectors)
    other_values, other_grad = swap(values), swap(grad_output)
    segment = jnp.concatenate([segment_index, other_segment])
    bias = jnp.where(segment[:, None] <= segment[None, :], 0.0, HIDDEN).astype(jnp.float32)
    out = jax.ShapeDtypeStruct((row_count, width), jnp.bfloat16)
    whole = pl.BlockSpec(memory_space=pltpu.VMEM)
    return pl.pallas_call(
        functools.partial(pair_kernel, width // HEAD_DIM, row_count),
        out_shape=(out,) * 4,
        in_specs=[whole] * 9,
        out_specs=(whole,) * 4,
    )(
        bias,
        queries,
        key_vectors,
        values,
        grad_output,
        other_queries,
        other_keys,
        other_values,
        other_grad,
    )


def solution(mesh):
    in_specs = (
        P(("dp", "frames"), "heads"),
        P(("dp", "frames"), "heads"),
        P(("dp", "frames"), "heads"),
        P(("dp", "frames"), "heads"),
        P(("dp", "frames")),
    )
    out_specs = (
        P(("dp", "frames"), "heads"),
        P(("dp", "frames"), "heads"),
        P(("dp", "frames"), "heads"),
        P(("dp", "frames"), "heads"),
    )
    body = pair_body if mesh.shape["frames"] == 2 else shards
    return jax.shard_map(body, mesh=mesh, in_specs=in_specs, out_specs=out_specs, check_vma=False)
```

```python
import functools
import math

import jax
import jax.numpy as jnp
from jax import lax
from jax.experimental import pallas as pl
from jax.experimental.pallas import tpu as pltpu
from jax.sharding import PartitionSpec as P

HEAD_DIM = 128


def head_split(array):
    return array.reshape(array.shape[0], array.shape[1] // HEAD_DIM, HEAD_DIM)


def natural_order(array, shard_count, row_count):
    half_rows = row_count // 2
    parts = array.reshape((shard_count, 2, half_rows) + array.shape[1:])
    joined = jnp.concatenate([parts[:, 0], jnp.flip(parts[:, 1], axis=0)], axis=0)
    return joined.reshape((shard_count * row_count,) + array.shape[1:])


def score_block(query_heads, key_heads):
    product = jnp.einsum("qhd,khd->qhk", query_heads, key_heads, preferred_element_type=jnp.float32)
    return product * (1.0 / math.sqrt(HEAD_DIM))


def visible(query_segment, key_segment):
    return key_segment[None, None, :] <= query_segment[:, None, None]


def weights_of(query_heads, query_segment, log_total, key_heads, key_segment):
    scores = score_block(query_heads, key_heads)
    return jnp.where(
        visible(query_segment, key_segment), jnp.exp(scores - log_total[:, :, None]), 0.0
    )


def grad_parts(
    query_heads,
    grad_heads,
    query_segment,
    log_total,
    row_delta,
    key_heads,
    value_heads,
    key_segment,
):
    soft_weights = weights_of(query_heads, query_segment, log_total, key_heads, key_segment)
    grad_weights = jnp.einsum(
        "qhd,khd->qhk", grad_heads, value_heads, preferred_element_type=jnp.float32
    )
    grad_scores = (soft_weights * (grad_weights - row_delta[:, :, None])).astype(jnp.bfloat16)
    return (soft_weights.astype(jnp.bfloat16), grad_scores)


def shards(queries, key_vectors, values, grad_output, segment_index):
    row_count, full_width = queries.shape
    head_count = full_width // HEAD_DIM
    shard_count = lax.axis_size("frames")
    scale_factor = 1.0 / math.sqrt(HEAD_DIM)
    query_heads = head_split(queries)
    grad_heads = head_split(grad_output)
    own_segment = segment_index.astype(jnp.float32)
    own_top = jnp.max(own_segment)
    own_bottom = jnp.min(own_segment)
    segment_tags = segment_index.astype(jnp.bfloat16)
    key_whole, value_whole, key_tags = (
        lax.all_gather(key_vectors, "frames", axis=0, tiled=True),
        lax.all_gather(values, "frames", axis=0, tiled=True),
        lax.all_gather(segment_tags, "frames", axis=0, tiled=True),
    )
    key_total = key_whole.shape[0]
    key_span = min(key_total, 4 * row_count)
    span_count = key_total // key_span
    key_heads_all = head_split(natural_order(key_whole, shard_count, row_count))
    value_heads_all = head_split(natural_order(value_whole, shard_count, row_count))
    key_segment_all = natural_order(key_tags, shard_count, row_count).astype(jnp.float32)

    def key_slice(block_index):
        first_row = block_index * key_span
        return (
            lax.dynamic_slice_in_dim(key_heads_all, first_row, key_span, 0),
            lax.dynamic_slice_in_dim(value_heads_all, first_row, key_span, 0),
            lax.dynamic_slice_in_dim(key_segment_all, first_row, key_span, 0),
        )

    def span_seen(key_segment):
        return jnp.min(key_segment) <= own_top

    def stats_step(block_index, loop_state):
        key_heads, value_heads, key_segment = key_slice(block_index)

        def stats_work(state):
            running_max, running_sum = state
            seen_mask = visible(own_segment, key_segment)
            scores = jnp.where(seen_mask, score_block(query_heads, key_heads), -1e30)
            new_max = jnp.maximum(running_max, jnp.max(scores, axis=2))
            added = jnp.sum(
                jnp.where(seen_mask, jnp.exp(scores - new_max[:, :, None]), 0.0), axis=2
            )
            return (new_max, running_sum * jnp.exp(running_max - new_max) + added)

        return lax.cond(span_seen(key_segment), stats_work, lambda state: state, loop_state)

    start_max = jnp.full((row_count, head_count), -1e30, jnp.float32)
    start_sum = jnp.zeros((row_count, head_count), jnp.float32)
    running_max, running_sum = lax.fori_loop(0, span_count, stats_step, (start_max, start_sum))
    log_total = running_max + jnp.log(running_sum)

    def output_step(block_index, total_acc):
        key_heads, value_heads, key_segment = key_slice(block_index)

        def output_work(acc):
            weights_low = weights_of(
                query_heads, own_segment, log_total, key_heads, key_segment
            ).astype(jnp.bfloat16)
            return acc + jnp.einsum(
                "qhk,khd->qhd", weights_low, value_heads, preferred_element_type=jnp.float32
            )

        return lax.cond(span_seen(key_segment), output_work, lambda acc: acc, total_acc)

    zero_rows = jnp.zeros((row_count, head_count, HEAD_DIM), jnp.float32)
    attended = (
        lax.fori_loop(0, span_count, output_step, zero_rows)
        .reshape(row_count, full_width)
        .astype(jnp.bfloat16)
    )
    row_delta = jnp.sum(
        grad_heads.astype(jnp.float32) * head_split(attended).astype(jnp.float32), axis=2
    )

    def query_grad_step(block_index, total_acc):
        key_heads, value_heads, key_segment = key_slice(block_index)

        def query_work(acc):
            weights_low, grad_scores = grad_parts(
                query_heads,
                grad_heads,
                own_segment,
                log_total,
                row_delta,
                key_heads,
                value_heads,
                key_segment,
            )
            return acc + jnp.einsum(
                "qhk,khd->qhd", grad_scores, key_heads, preferred_element_type=jnp.float32
            )

        return lax.cond(span_seen(key_segment), query_work, lambda acc: acc, total_acc)

    query_acc = lax.fori_loop(0, span_count, query_grad_step, zero_rows)
    grad_queries = (query_acc * scale_factor).reshape(row_count, full_width).astype(jnp.bfloat16)
    query_whole, grad_whole, query_tags = (
        lax.all_gather(queries, "frames", axis=0, tiled=True),
        lax.all_gather(grad_output, "frames", axis=0, tiled=True),
        lax.all_gather(segment_tags, "frames", axis=0, tiled=True),
    )
    total_whole, delta_whole = (
        lax.all_gather(log_total, "frames", axis=0, tiled=True),
        lax.all_gather(row_delta, "frames", axis=0, tiled=True),
    )
    query_heads_all = head_split(natural_order(query_whole, shard_count, row_count))
    grad_heads_all = head_split(natural_order(grad_whole, shard_count, row_count))
    query_segment_all = natural_order(query_tags, shard_count, row_count).astype(jnp.float32)
    total_all = natural_order(total_whole, shard_count, row_count)
    delta_all = natural_order(delta_whole, shard_count, row_count)
    own_keys = head_split(key_vectors)
    own_values = head_split(values)

    def key_grad_step(block_index, loop_state):
        first_row = block_index * key_span
        block_queries = lax.dynamic_slice_in_dim(query_heads_all, first_row, key_span, 0)
        block_grads = lax.dynamic_slice_in_dim(grad_heads_all, first_row, key_span, 0)
        block_segment = lax.dynamic_slice_in_dim(query_segment_all, first_row, key_span, 0)
        block_total = lax.dynamic_slice_in_dim(total_all, first_row, key_span, 0)
        block_delta = lax.dynamic_slice_in_dim(delta_all, first_row, key_span, 0)

        def key_work(state):
            key_acc, value_acc = state
            weights_low, grad_scores = grad_parts(
                block_queries,
                block_grads,
                block_segment,
                block_total,
                block_delta,
                own_keys,
                own_values,
                own_segment,
            )
            key_acc = key_acc + jnp.einsum(
                "qhk,qhd->khd", grad_scores, block_queries, preferred_element_type=jnp.float32
            )
            value_acc = value_acc + jnp.einsum(
                "qhk,qhd->khd", weights_low, block_grads, preferred_element_type=jnp.float32
            )
            return (key_acc, value_acc)

        return lax.cond(
            jnp.max(block_segment) >= own_bottom, key_work, lambda state: state, loop_state
        )

    key_acc, value_acc = lax.fori_loop(0, span_count, key_grad_step, (zero_rows, zero_rows))
    grad_keys = (key_acc * scale_factor).reshape(row_count, full_width).astype(jnp.bfloat16)
    grad_values = value_acc.reshape(row_count, full_width).astype(jnp.bfloat16)
    return (attended, grad_queries, grad_keys, grad_values)


HIDDEN = -1e30
LANES = 128
CHUNK = 80
NT = (((1,), (1,)), ((), ()))
TN = (((0,), (0,)), ((), ()))
NN = (((1,), (0,)), ((), ()))
PLAN = ((("S", 0), ("M", 1)), (("P", 1), ("B", 2)), (("C", 4), ("E", 3)))


def dot(left, right, dims):
    return lax.dot_general(left, right, dims, preferred_element_type=jnp.float32)


def cols(head, count=1):
    return slice(head * HEAD_DIM, (head + count) * HEAD_DIM)


def side_by_side(generators):
    generators = list(generators)
    while generators:
        generators = [item for item in generators if next(item, None) is not None]


def stack_rows(first, second, head, count=1):
    return jnp.concatenate([first[:, cols(head, count)], second[:, cols(head, count)]], axis=0)


def load_kernel(*refs):
    count = (len(refs) - 1) // 2
    copies = [
        pltpu.make_async_copy(source, target, refs[-1].at[at])
        for at, (source, target) in enumerate(zip(refs[:count], refs[count:]))
    ]
    for copy in copies:
        copy.start()
    for copy in copies:
        copy.wait()


def load_early(arrays):
    arrays = tuple(pltpu.with_memory_space_constraint(array, pltpu.HBM) for array in arrays)
    count = len(arrays)
    return pl.pallas_call(
        load_kernel,
        out_shape=tuple(jax.ShapeDtypeStruct(array.shape, array.dtype) for array in arrays),
        in_specs=[pl.BlockSpec(memory_space=pl.ANY)] * count,
        out_specs=(pl.BlockSpec(memory_space=pltpu.VMEM),) * count,
        scratch_shapes=[pltpu.SemaphoreType.DMA((count,))],
        compiler_params=pltpu.CompilerParams(vmem_limit_bytes=4 * 1024 * 1024),
        cost_estimate=pl.CostEstimate(
            flops=0, transcendentals=0, bytes_accessed=2 * sum(a.size * 2 for a in arrays)
        ),
    )(*arrays)


def pair_kernel(
    heads, rows,
    s0, s1, q0, k0, v0, g0, q1, k1, v1, g1,
    o_hbm, dq_hbm, dk_hbm, dv_hbm,
    bias_ref, o_ref, dq_ref, dk_ref, dv_ref, sem,
):
    scale = 1.0 / math.sqrt(HEAD_DIM)
    scale_two = scale * math.log2(math.e)
    total = 2 * rows
    own_rest = rows - LANES
    rest = 2 * own_rest
    low_type = jnp.bfloat16

    key_segment = jnp.concatenate([s0[...], s1[...]], axis=1)
    tails = [s0[:, LANES:], s1[:, LANES:]]
    query_segment = jnp.concatenate([s0[:, :LANES], s1[:, :LANES]] + tails + tails, axis=1)
    key_column = jnp.transpose(jnp.broadcast_to(key_segment, (8, total)))[:, :1]
    bias_ref[...] = jnp.where(key_column <= query_segment, 0.0, HIDDEN)

    zero = jnp.zeros((rest, HEAD_DIM), low_type)

    def tail_rows(first, second, head):
        return jnp.concatenate([first[LANES:, cols(head)], second[LANES:, cols(head)]], axis=0)

    def strip_rows(first, second, kind, head):
        if kind == 0:
            return first[:LANES, cols(head)]
        if kind == 1:
            return second[:LANES, cols(head)]
        upper = jnp.concatenate([tail_rows(first, second, head), zero], axis=1)
        lower = jnp.concatenate([zero, tail_rows(first, second, head + 1)], axis=1)
        return jnp.concatenate([upper, lower], axis=0)

    strips = []
    for head in range(0, heads, 2):
        strips += [(0, head), (1, head), (2, head), (0, head + 1), (1, head + 1)]
    per_pair = 5
    chunks = [(low, min(low + CHUNK, total)) for low in range(0, total, CHUNK)]
    state = [dict() for _ in strips]
    sums = {}
    outputs = ((o_ref, o_hbm), (dq_ref, dq_hbm), (dk_ref, dk_hbm), (dv_ref, dv_hbm))

    def fold(function, block):
        return function(block.reshape(block.shape[0] // 8, 8, LANES), axis=0)

    def add_to(name, head, part):
        sums[name, head] = sums[name, head] + part if (name, head) in sums else part

    def copy_out(at, head):
        source, target = outputs[at]
        span = cols(head, 2)
        return pltpu.make_async_copy(
            source.at[:, span], target.at[:, span], sem.at[at, head // 2]
        )

    def scores_stage(at):
        kind, head = strips[at]
        count = 2 if kind == 2 else 1
        state[at]["s"] = dot(
            stack_rows(k0, k1, head, count), strip_rows(q0, q1, kind, head), NT
        )
        yield True

    def mask_stage(at):
        kind, head = strips[at]
        scores = state[at].pop("s")
        masked, top = [], None
        for low, high in chunks:
            block = scores[low:high] + bias_ref[low:high, kind * LANES : (kind + 1) * LANES]
            masked.append(block)
            part = fold(jnp.max, block)
            top = part if top is None else jnp.maximum(top, part)
            yield True
        state[at].update(masked=masked, top=jnp.max(top, axis=0, keepdims=True))

    def products_stage(at):
        kind, head = strips[at]
        count = 2 if kind == 2 else 1
        state[at]["dp"] = dot(
            stack_rows(v0, v1, head, count), strip_rows(g0, g1, kind, head), NT
        )
        yield True

    def softmax_stage(at):
        top, masked, products = state[at].pop("top"), state[at].pop("masked"), state[at]["dp"]
        raws, norm, delta = [], None, None
        for (low, high), block in zip(chunks, masked):
            raw = jnp.exp2((block - top) * scale_two)
            raws.append(raw)
            norm_part, delta_part = fold(jnp.sum, raw), fold(jnp.sum, raw * products[low:high])
            norm = norm_part if norm is None else norm + norm_part
            delta = delta_part if delta is None else delta + delta_part
            yield True
        inverse = 1.0 / jnp.sum(norm, axis=0, keepdims=True)
        delta = jnp.sum(delta, axis=0, keepdims=True) * inverse
        state[at].update(raws=raws, inverse=inverse, delta=delta)

    def weights_stage(at):
        kind, head = strips[at]
        inverse, delta, raws, products = (
            state[at].pop(name) for name in ("inverse", "delta", "raws", "dp")
        )
        weights, grads = [], []
        for (low, high), raw in zip(chunks, raws):
            if kind == 1 and low >= rows:
                continue
            soft = raw * inverse
            weights.append(soft.astype(low_type))
            grads.append((soft * (products[low:high] - delta)).astype(low_type))
            yield True
        state[at].update(
            low=jnp.concatenate(weights, axis=0), ds=jnp.concatenate(grads, axis=0)
        )

    def outputs_stage(at):
        kind, head = strips[at]
        low, ds = state[at].pop("low"), state[at].pop("ds")
        if kind < 2:
            add_to("v", head, dot(low[:rows], strip_rows(g0, g1, kind, head), NN))
            yield True
            add_to("k", head, dot(ds[:rows], strip_rows(q0, q1, kind, head), NN))
            yield True
        if kind == 0:
            o_ref[:LANES, cols(head)] = dot(low, stack_rows(v0, v1, head), TN).astype(low_type)
            yield True
            part = dot(ds, stack_rows(k0, k1, head), TN) * scale
            dq_ref[:LANES, cols(head)] = part.astype(low_type)
            yield True
        if kind == 2:
            for side in range(2):
                span = cols(side)
                add_to("v", head + side, dot(low[:rows], strip_rows(g0, g1, 2, head)[:, span], NN))
                yield True
                add_to("k", head + side, dot(ds[:rows], strip_rows(q0, q1, 2, head)[:, span], NN))
                yield True
            low_turned, ds_turned = jnp.transpose(low), jnp.transpose(ds)
            for side in range(2):
                mine = slice(side * rest, side * rest + own_rest)
                span = cols(head + side)
                part = dot(low_turned[mine], stack_rows(v0, v1, head + side), NN)
                o_ref[LANES:, span] = part.astype(low_type)
                part = dot(ds_turned[mine], stack_rows(k0, k1, head + side), NN) * scale
                dq_ref[LANES:, span] = part.astype(low_type)
                yield True
        if at % per_pair == per_pair - 1:
            for member in (head - 1, head):
                dk_ref[:, cols(member)] = (sums.pop(("k", member)) * scale).astype(low_type)
                dv_ref[:, cols(member)] = sums.pop(("v", member)).astype(low_type)
            for output in range(len(outputs)):
                copy_out(output, head - 1).start()
        yield True

    stages = dict(
        S=scores_stage,
        M=mask_stage,
        P=products_stage,
        B=softmax_stage,
        E=weights_stage,
        C=outputs_stage,
    )
    last_lag = max(lag for group in PLAN for _, lag in group)
    for step in range(len(strips) + last_lag):
        for group in PLAN:
            side_by_side(
                stages[name](step - lag) for name, lag in group if 0 <= step - lag < len(strips)
            )
    for head in range(0, heads, 2):
        for output in range(len(outputs)):
            copy_out(output, head).wait()


def pair_body(queries, key_vectors, values, grad_output, segment_index):
    rows, width = queries.shape
    heads = width // HEAD_DIM

    def swap(array):
        return lax.ppermute(array, "frames", [(0, 1), (1, 0)])

    other_keys, other_queries = swap(key_vectors), swap(queries)
    other_values, other_grad = swap(values), swap(grad_output)
    other_segment = swap(segment_index).reshape(1, rows)
    own = load_early((segment_index.reshape(1, rows), queries, key_vectors, values, grad_output))
    out = jax.ShapeDtypeStruct((rows, width), jnp.bfloat16)
    on_chip = pl.BlockSpec(memory_space=pltpu.VMEM)
    return pl.pallas_call(
        functools.partial(pair_kernel, heads, rows),
        out_shape=(out,) * 4,
        in_specs=[on_chip] * 10,
        out_specs=(pl.BlockSpec(memory_space=pl.ANY),) * 4,
        scratch_shapes=[pltpu.VMEM((2 * rows, 3 * LANES), jnp.float32)]
        + [pltpu.VMEM((rows, width), jnp.bfloat16)] * 4
        + [pltpu.SemaphoreType.DMA((4, heads // 2))],
        compiler_params=pltpu.CompilerParams(vmem_limit_bytes=32 * 1024 * 1024),
    )(own[0], other_segment, *own[1:], other_queries, other_keys, other_values, other_grad)


def pair_fits(rows, width):
    return 4 * (rows - LANES) == LANES and width % (2 * HEAD_DIM) == 0


def plan_for_shapes(queries, key_vectors, values, grad_output, segment_index):
    paired = lax.axis_size("frames") == 2 and pair_fits(*queries.shape)
    body = pair_body if paired else shards
    return body(queries, key_vectors, values, grad_output, segment_index)


def solution(mesh):
    in_specs = (
        P(("dp", "frames"), "heads"),
        P(("dp", "frames"), "heads"),
        P(("dp", "frames"), "heads"),
        P(("dp", "frames"), "heads"),
        P(("dp", "frames")),
    )
    out_specs = (
        P(("dp", "frames"), "heads"),
        P(("dp", "frames"), "heads"),
        P(("dp", "frames"), "heads"),
        P(("dp", "frames"), "heads"),
    )
    return jax.shard_map(
        plan_for_shapes, mesh=mesh, in_specs=in_specs, out_specs=out_specs, check_vma=False
    )
```

```python
import functools
import math

import jax
import jax.numpy as jnp
from jax import lax
from jax.experimental import pallas as pl
from jax.experimental.pallas import tpu as pltpu
from jax.sharding import PartitionSpec as P

HEAD_DIM = 128


def head_split(array):
    return array.reshape(array.shape[0], array.shape[1] // HEAD_DIM, HEAD_DIM)


def natural_order(array, shard_count, row_count):
    half_rows = row_count // 2
    parts = array.reshape((shard_count, 2, half_rows) + array.shape[1:])
    joined = jnp.concatenate([parts[:, 0], jnp.flip(parts[:, 1], axis=0)], axis=0)
    return joined.reshape((shard_count * row_count,) + array.shape[1:])


def score_block(query_heads, key_heads):
    product = jnp.einsum("qhd,khd->qhk", query_heads, key_heads, preferred_element_type=jnp.float32)
    return product * (1.0 / math.sqrt(HEAD_DIM))


def visible(query_segment, key_segment):
    return key_segment[None, None, :] <= query_segment[:, None, None]


def weights_of(query_heads, query_segment, log_total, key_heads, key_segment):
    scores = score_block(query_heads, key_heads)
    return jnp.where(
        visible(query_segment, key_segment), jnp.exp(scores - log_total[:, :, None]), 0.0
    )


def grad_parts(
    query_heads,
    grad_heads,
    query_segment,
    log_total,
    row_delta,
    key_heads,
    value_heads,
    key_segment,
):
    soft_weights = weights_of(query_heads, query_segment, log_total, key_heads, key_segment)
    grad_weights = jnp.einsum(
        "qhd,khd->qhk", grad_heads, value_heads, preferred_element_type=jnp.float32
    )
    grad_scores = (soft_weights * (grad_weights - row_delta[:, :, None])).astype(jnp.bfloat16)
    return (soft_weights.astype(jnp.bfloat16), grad_scores)


def shards(queries, key_vectors, values, grad_output, segment_index):
    row_count, full_width = queries.shape
    head_count = full_width // HEAD_DIM
    shard_count = lax.axis_size("frames")
    scale_factor = 1.0 / math.sqrt(HEAD_DIM)
    query_heads = head_split(queries)
    grad_heads = head_split(grad_output)
    own_segment = segment_index.astype(jnp.float32)
    own_top = jnp.max(own_segment)
    own_bottom = jnp.min(own_segment)
    segment_tags = segment_index.astype(jnp.bfloat16)
    key_whole, value_whole, key_tags = (
        lax.all_gather(key_vectors, "frames", axis=0, tiled=True),
        lax.all_gather(values, "frames", axis=0, tiled=True),
        lax.all_gather(segment_tags, "frames", axis=0, tiled=True),
    )
    key_total = key_whole.shape[0]
    key_span = min(key_total, 4 * row_count)
    span_count = key_total // key_span
    key_heads_all = head_split(natural_order(key_whole, shard_count, row_count))
    value_heads_all = head_split(natural_order(value_whole, shard_count, row_count))
    key_segment_all = natural_order(key_tags, shard_count, row_count).astype(jnp.float32)

    def key_slice(block_index):
        first_row = block_index * key_span
        return (
            lax.dynamic_slice_in_dim(key_heads_all, first_row, key_span, 0),
            lax.dynamic_slice_in_dim(value_heads_all, first_row, key_span, 0),
            lax.dynamic_slice_in_dim(key_segment_all, first_row, key_span, 0),
        )

    def span_seen(key_segment):
        return jnp.min(key_segment) <= own_top

    def stats_step(block_index, loop_state):
        key_heads, _, key_segment = key_slice(block_index)

        def stats_work(state):
            running_max, running_sum = state
            seen_mask = visible(own_segment, key_segment)
            scores = jnp.where(seen_mask, score_block(query_heads, key_heads), -1e30)
            new_max = jnp.maximum(running_max, jnp.max(scores, axis=2))
            added = jnp.sum(
                jnp.where(seen_mask, jnp.exp(scores - new_max[:, :, None]), 0.0), axis=2
            )
            return (new_max, running_sum * jnp.exp(running_max - new_max) + added)

        return lax.cond(span_seen(key_segment), stats_work, lambda state: state, loop_state)

    start_max = jnp.full((row_count, head_count), -1e30, jnp.float32)
    start_sum = jnp.zeros((row_count, head_count), jnp.float32)
    running_max, running_sum = lax.fori_loop(0, span_count, stats_step, (start_max, start_sum))
    log_total = running_max + jnp.log(running_sum)

    def output_step(block_index, total_acc):
        key_heads, value_heads, key_segment = key_slice(block_index)

        def output_work(acc):
            weights_low = weights_of(
                query_heads, own_segment, log_total, key_heads, key_segment
            ).astype(jnp.bfloat16)
            return acc + jnp.einsum(
                "qhk,khd->qhd", weights_low, value_heads, preferred_element_type=jnp.float32
            )

        return lax.cond(span_seen(key_segment), output_work, lambda acc: acc, total_acc)

    zero_rows = jnp.zeros((row_count, head_count, HEAD_DIM), jnp.float32)
    attended = (
        lax.fori_loop(0, span_count, output_step, zero_rows)
        .reshape(row_count, full_width)
        .astype(jnp.bfloat16)
    )
    row_delta = jnp.sum(
        grad_heads.astype(jnp.float32) * head_split(attended).astype(jnp.float32), axis=2
    )

    def query_grad_step(block_index, total_acc):
        key_heads, value_heads, key_segment = key_slice(block_index)

        def query_work(acc):
            _, grad_scores = grad_parts(
                query_heads,
                grad_heads,
                own_segment,
                log_total,
                row_delta,
                key_heads,
                value_heads,
                key_segment,
            )
            return acc + jnp.einsum(
                "qhk,khd->qhd", grad_scores, key_heads, preferred_element_type=jnp.float32
            )

        return lax.cond(span_seen(key_segment), query_work, lambda acc: acc, total_acc)

    query_acc = lax.fori_loop(0, span_count, query_grad_step, zero_rows)
    grad_queries = (query_acc * scale_factor).reshape(row_count, full_width).astype(jnp.bfloat16)
    query_whole, grad_whole, query_tags = (
        lax.all_gather(queries, "frames", axis=0, tiled=True),
        lax.all_gather(grad_output, "frames", axis=0, tiled=True),
        lax.all_gather(segment_tags, "frames", axis=0, tiled=True),
    )
    total_whole, delta_whole = (
        lax.all_gather(log_total, "frames", axis=0, tiled=True),
        lax.all_gather(row_delta, "frames", axis=0, tiled=True),
    )
    query_heads_all = head_split(natural_order(query_whole, shard_count, row_count))
    grad_heads_all = head_split(natural_order(grad_whole, shard_count, row_count))
    query_segment_all = natural_order(query_tags, shard_count, row_count).astype(jnp.float32)
    total_all = natural_order(total_whole, shard_count, row_count)
    delta_all = natural_order(delta_whole, shard_count, row_count)
    own_keys = head_split(key_vectors)
    own_values = head_split(values)

    def key_grad_step(block_index, loop_state):
        first_row = block_index * key_span
        block_queries = lax.dynamic_slice_in_dim(query_heads_all, first_row, key_span, 0)
        block_grads = lax.dynamic_slice_in_dim(grad_heads_all, first_row, key_span, 0)
        block_segment = lax.dynamic_slice_in_dim(query_segment_all, first_row, key_span, 0)
        block_total = lax.dynamic_slice_in_dim(total_all, first_row, key_span, 0)
        block_delta = lax.dynamic_slice_in_dim(delta_all, first_row, key_span, 0)

        def key_work(state):
            key_acc, value_acc = state
            weights_low, grad_scores = grad_parts(
                block_queries,
                block_grads,
                block_segment,
                block_total,
                block_delta,
                own_keys,
                own_values,
                own_segment,
            )
            key_acc = key_acc + jnp.einsum(
                "qhk,qhd->khd", grad_scores, block_queries, preferred_element_type=jnp.float32
            )
            value_acc = value_acc + jnp.einsum(
                "qhk,qhd->khd", weights_low, block_grads, preferred_element_type=jnp.float32
            )
            return (key_acc, value_acc)

        return lax.cond(
            jnp.max(block_segment) >= own_bottom, key_work, lambda state: state, loop_state
        )

    key_acc, value_acc = lax.fori_loop(0, span_count, key_grad_step, (zero_rows, zero_rows))
    grad_keys = (key_acc * scale_factor).reshape(row_count, full_width).astype(jnp.bfloat16)
    grad_values = value_acc.reshape(row_count, full_width).astype(jnp.bfloat16)
    return (attended, grad_queries, grad_keys, grad_values)


HIDDEN = -1e30
LANES = 128
CHUNK = 80
NT = (((1,), (1,)), ((), ()))
TN = (((0,), (0,)), ((), ()))
NN = (((1,), (0,)), ((), ()))
PLAN = ((("S", 0),), (("C", 5),), (("P", 0),), (("M", 1),), (("B", 2),), (("E", 3),))


def dot(left, right, dims):
    return lax.dot_general(left, right, dims, preferred_element_type=jnp.float32)


def cols(head, count=1):
    return slice(head * HEAD_DIM, (head + count) * HEAD_DIM)


def side_by_side(generators):
    generators = list(generators)
    while generators:
        generators = [item for item in generators if next(item, None) is not None]


def stack_rows(first, second, head, count=1):
    return jnp.concatenate([first[:, cols(head, count)], second[:, cols(head, count)]], axis=0)


def load_kernel(*refs):
    *sources, segment, stacked, own_segment, sem = refs
    for at, source in enumerate(sources):
        pltpu.make_async_copy(source, stacked.at[at], sem.at[0]).start()
    segment_copy = pltpu.make_async_copy(segment, own_segment, sem.at[1])
    segment_copy.start()
    segment_copy.wait()
    pltpu.make_async_copy(stacked, stacked, sem.at[0]).wait()


def load_early(arrays, segment):
    arrays = tuple(pltpu.with_memory_space_constraint(a, pltpu.HBM) for a in arrays + (segment,))
    count = len(arrays)
    stacked = jax.ShapeDtypeStruct((count - 1,) + arrays[0].shape, arrays[0].dtype)
    return pl.pallas_call(
        load_kernel,
        out_shape=(stacked, jax.ShapeDtypeStruct(segment.shape, segment.dtype)),
        in_specs=[pl.BlockSpec(memory_space=pl.ANY)] * count,
        out_specs=(pl.BlockSpec(memory_space=pltpu.VMEM),) * 2,
        scratch_shapes=[pltpu.SemaphoreType.DMA((2,))],
        compiler_params=pltpu.CompilerParams(vmem_limit_bytes=4 * 1024 * 1024),
        cost_estimate=pl.CostEstimate(
            flops=0, transcendentals=0, bytes_accessed=4 * stacked.size
        ),
    )(*arrays)


def fill_mask(bias_ref, s0, s1, query_segment):
    key_segment = jnp.concatenate([s0[...], s1[...]], axis=1)
    key_column = jnp.transpose(jnp.broadcast_to(key_segment, (8, key_segment.shape[1])))[:, :1]
    bias_ref[...] = jnp.where(key_column <= query_segment, 0.0, HIDDEN)


def run_strips(strips, rows, operands, bias_of, outputs_stage):
    scale_two = math.log2(math.e) / math.sqrt(HEAD_DIM)
    total = 2 * rows
    q0, k0, v0, g0, q1, k1, v1, g1 = operands
    chunks = [(low, min(low + CHUNK, total)) for low in range(0, total, CHUNK)]
    state = [dict() for _ in strips]

    def fold(function, block):
        return function(block.reshape(block.shape[0] // 8, 8, LANES), axis=0)

    def scores_stage(at):
        kind, head = strips[at]
        count = 2 if kind == "tail" else 1
        state[at]["s"] = dot(
            stack_rows(k0, k1, head, count), strip_rows(q0, q1, kind, head), NT
        )
        yield True

    def mask_stage(at):
        scores, bias = state[at].pop("s"), bias_of(strips[at][0])
        masked, top = [], None
        for low, high in chunks:
            block = scores[low:high] + bias[low:high]
            masked.append(block)
            part = fold(jnp.max, block)
            top = part if top is None else jnp.maximum(top, part)
            yield True
        state[at].update(masked=masked, top=jnp.max(top, axis=0, keepdims=True))

    def products_stage(at):
        kind, head = strips[at]
        count = 2 if kind == "tail" else 1
        state[at]["dp"] = dot(
            stack_rows(v0, v1, head, count), strip_rows(g0, g1, kind, head), NT
        )
        yield True

    def softmax_stage(at):
        top, masked, products = state[at].pop("top"), state[at].pop("masked"), state[at]["dp"]
        raws, norm, delta = [], None, None
        for (low, high), block in zip(chunks, masked):
            raw = jnp.exp2((block - top) * scale_two)
            raws.append(raw)
            norm_part, delta_part = fold(jnp.sum, raw), fold(jnp.sum, raw * products[low:high])
            norm = norm_part if norm is None else norm + norm_part
            delta = delta_part if delta is None else delta + delta_part
            yield True
        inverse = 1.0 / jnp.sum(norm, axis=0, keepdims=True)
        delta = jnp.sum(delta, axis=0, keepdims=True) * inverse
        state[at].update(raws=raws, inverse=inverse, delta=delta)

    def weights_stage(at):
        inverse, delta, raws, products = (
            state[at].pop(name) for name in ("inverse", "delta", "raws", "dp")
        )
        weights, grads = [], []
        for (low, high), raw in zip(chunks, raws):
            if strips[at][0] == "other" and low >= rows:
                continue
            soft = raw * inverse
            weights.append(soft.astype(jnp.bfloat16))
            grads.append((soft * (products[low:high] - delta)).astype(jnp.bfloat16))
            yield True
        state[at].update(
            low=jnp.concatenate(weights, axis=0), ds=jnp.concatenate(grads, axis=0)
        )

    def last_stage(at):
        yield from outputs_stage(*strips[at], state[at].pop("low"), state[at].pop("ds"))

    stages = dict(
        S=scores_stage,
        M=mask_stage,
        P=products_stage,
        B=softmax_stage,
        E=weights_stage,
        C=last_stage,
    )
    last_lag = max(lag for group in PLAN for _, lag in group)
    for step in range(len(strips) + last_lag):
        for group in PLAN:
            side_by_side(
                stages[name](step - lag) for name, lag in group if 0 <= step - lag < len(strips)
            )


def tail_rows(first, second, head):
    return jnp.concatenate([first[LANES:, cols(head)], second[LANES:, cols(head)]], axis=0)


def strip_rows(first, second, kind, head):
    if kind == "own":
        return first[:LANES, cols(head)]
    if kind == "other":
        return second[:LANES, cols(head)]
    own, beside = tail_rows(first, second, head), tail_rows(first, second, head + 1)
    zero = jnp.zeros_like(own)
    upper = jnp.concatenate([own, zero], axis=1)
    return jnp.concatenate([upper, jnp.concatenate([zero, beside], axis=1)], axis=0)


def own_kernel(
    heads, rows, s0, s1, own, k1, v1, o_ref, dq_ref, dk_ref, dv_ref, bias_ref
):
    q0, k0, v0, g0 = (own.at[at] for at in range(4))
    scale = 1.0 / math.sqrt(HEAD_DIM)
    fill_mask(bias_ref, s0, s1, s0[:, :LANES])

    def outputs(kind, head, low, ds):
        span = cols(head)
        dv_ref[:, span] = dot(low[:rows], g0[:LANES, span], NN)
        yield True
        dk_ref[:, span] = dot(ds[:rows], q0[:LANES, span], NN)
        yield True
        o_ref[:, span] = dot(low, stack_rows(v0, v1, head), TN).astype(jnp.bfloat16)
        yield True
        part = dot(ds, stack_rows(k0, k1, head), TN) * scale
        dq_ref[:, span] = part.astype(jnp.bfloat16)
        yield True

    strips = [("own", head) for head in range(heads)]
    operands = (q0, k0, v0, g0, None, k1, v1, None)
    run_strips(strips, rows, operands, lambda kind: bias_ref, outputs)


def rest_kernel(
    heads, rows,
    s0, s1, own, q1, k1, v1, g1, o_own, dq_own, dk_own, dv_own,
    o_hbm, dq_hbm, dk_hbm, dv_hbm,
    bias_ref, o_ref, dq_ref, dk_ref, dv_ref, sem,
):
    scale = 1.0 / math.sqrt(HEAD_DIM)
    q0, k0, v0, g0 = (own.at[at] for at in range(4))
    own_rest = rows - LANES
    rest = 2 * own_rest

    for at, (source, target) in enumerate(((o_own, o_hbm), (dq_own, dq_hbm))):
        pltpu.make_async_copy(source, target.at[:LANES, :], sem.at[at]).start()

    def copy_out(at, head):
        source, target = (
            (o_ref, o_hbm.at[LANES:, :]),
            (dq_ref, dq_hbm.at[LANES:, :]),
            (dk_ref, dk_hbm),
            (dv_ref, dv_hbm),
        )[at]
        span = cols(head, 2)
        return pltpu.make_async_copy(source.at[:, span], target.at[:, span], sem.at[at])

    tails = [s0[:, LANES:], s1[:, LANES:]]
    fill_mask(bias_ref, s0, s1, jnp.concatenate([s1[:, :LANES]] + tails + tails, axis=1))

    def bias_of(kind):
        return bias_ref[:, :LANES] if kind == "other" else bias_ref[:, LANES:]

    tails_of = {}

    def query_rows(first, second, head):
        tail = tail_rows(first, second, head)
        zero = jnp.zeros_like(tail)
        parts = [second[:LANES, cols(head)]] + ([zero, tail] if head % 2 else [tail, zero])
        return jnp.concatenate(parts, axis=0)

    def outputs(kind, head, low, ds):
        if kind == "tail":
            low_turned, ds_turned = jnp.transpose(low), jnp.transpose(ds)
            for side in range(2):
                mine = slice(side * rest, side * rest + own_rest)
                span = cols(head + side)
                tails_of[head + side] = (low[:rows], ds[:rows])
                part = dot(low_turned[mine], stack_rows(v0, v1, head + side), NN)
                o_ref[:, span] = part.astype(jnp.bfloat16)
                part = dot(ds_turned[mine], stack_rows(k0, k1, head + side), NN) * scale
                dq_ref[:, span] = part.astype(jnp.bfloat16)
                yield True
            return
        span = cols(head)
        low_tail, ds_tail = tails_of.pop(head)
        part = dot(jnp.concatenate([low, low_tail], axis=1), query_rows(g0, g1, head), NN)
        dv_ref[:, span] = (part + dv_own[:, span]).astype(jnp.bfloat16)
        yield True
        part = dot(jnp.concatenate([ds, ds_tail], axis=1), query_rows(q0, q1, head), NN)
        dk_ref[:, span] = ((part + dk_own[:, span]) * scale).astype(jnp.bfloat16)
        if head % 2:
            for output in range(4):
                copy_out(output, head - 1).start()
        yield True

    strips = []
    for head in range(0, heads, 2):
        strips += [("tail", head), ("other", head), ("other", head + 1)]
    run_strips(strips, rows, (q0, k0, v0, g0, q1, k1, v1, g1), bias_of, outputs)
    for at, target in enumerate((o_hbm, dq_hbm, dk_hbm, dv_hbm)):
        pltpu.make_async_copy(dk_ref, target, sem.at[at]).wait()


def pair_body(queries, key_vectors, values, grad_output, segment_index):
    rows, width = queries.shape
    heads = width // HEAD_DIM

    def swap(array):
        return lax.ppermute(array, "frames", [(0, 1), (1, 0)])

    other_keys, other_values = swap(key_vectors), swap(values)
    other_segment = swap(segment_index).reshape(1, rows)
    other_queries, other_grad = swap(queries), swap(grad_output)
    own, own_segment = load_early(
        (queries, key_vectors, values, grad_output), segment_index.reshape(1, rows)
    )
    on_chip = pl.BlockSpec(memory_space=pltpu.VMEM)
    f32, bf16 = jnp.float32, jnp.bfloat16
    limit = 24 * 1024 * 1024
    partial_results = pl.pallas_call(
        functools.partial(own_kernel, heads, rows),
        out_shape=(
            jax.ShapeDtypeStruct((LANES, width), bf16),
            jax.ShapeDtypeStruct((LANES, width), bf16),
            jax.ShapeDtypeStruct((rows, width), f32),
            jax.ShapeDtypeStruct((rows, width), f32),
        ),
        in_specs=[on_chip] * 5,
        out_specs=(on_chip,) * 4,
        scratch_shapes=[pltpu.VMEM((2 * rows, LANES), f32)],
        compiler_params=pltpu.CompilerParams(vmem_limit_bytes=limit),
        cost_estimate=pl.CostEstimate(
            flops=12 * LANES * 2 * rows * width,
            transcendentals=0,
            bytes_accessed=12 * rows * width * 2,
        ),
    )(own_segment, other_segment, own, other_keys, other_values)
    return pl.pallas_call(
        functools.partial(rest_kernel, heads, rows),
        out_shape=(jax.ShapeDtypeStruct((rows, width), bf16),) * 4,
        in_specs=[on_chip] * 11,
        out_specs=(pl.BlockSpec(memory_space=pl.ANY),) * 4,
        scratch_shapes=[pltpu.VMEM((2 * rows, 2 * LANES), f32)]
        + [pltpu.VMEM((rows - LANES, width), bf16)] * 2
        + [pltpu.VMEM((rows, width), bf16)] * 2
        + [pltpu.SemaphoreType.DMA((4,))],
        compiler_params=pltpu.CompilerParams(vmem_limit_bytes=limit),
    )(
        own_segment,
        other_segment,
        own,
        other_queries,
        other_keys,
        other_values,
        other_grad,
        *partial_results,
    )


def pair_fits(rows, width):
    return 4 * (rows - LANES) == LANES and width % (2 * HEAD_DIM) == 0


def plan_for_shapes(queries, key_vectors, values, grad_output, segment_index):
    paired = lax.axis_size("frames") == 2 and pair_fits(*queries.shape)
    body = pair_body if paired else shards
    return body(queries, key_vectors, values, grad_output, segment_index)


def solution(mesh):
    in_specs = (
        P(("dp", "frames"), "heads"),
        P(("dp", "frames"), "heads"),
        P(("dp", "frames"), "heads"),
        P(("dp", "frames"), "heads"),
        P(("dp", "frames")),
    )
    out_specs = (
        P(("dp", "frames"), "heads"),
        P(("dp", "frames"), "heads"),
        P(("dp", "frames"), "heads"),
        P(("dp", "frames"), "heads"),
    )
    return jax.shard_map(
        plan_for_shapes, mesh=mesh, in_specs=in_specs, out_specs=out_specs, check_vma=False
    )
```
